768 devices in a mesh: blk: 192 (over y, z, core), grp: 4 (over x).
Axes of the slice: x: 4, y: 8, z: 12, core: 2. Of those that a mesh axis runs over, the one named last changes fastest.
Arguments:
- dual_rhs: float32 [4, 16, 196608], P('grp', None, 'blk'), may hold values from -32 to 32
- dual_ops: bfloat16 [4, 196608, 1024], P('grp', 'blk'), may hold values from -1 to 6, as said below
- prec_ops: bfloat16 [4, 196608, 1024], P('grp', 'blk'), may hold values from -1 to 4, as said below
- corner_coupling: bfloat16 [4, 4608, 512], P('grp', 'blk'), may hold values from -0.25 to 0.25
- corner_map: int32 [4, 4608], P('grp', 'blk'), may hold values from 0 to 767
- signs: int32 [4, 196608], P('grp', 'blk'), may hold values from -1 to 1, as said below
- coarse_inverse: float32 [768, 768], replicated, may hold values from -1 to 5, as said below
Outputs:
- multipliers: float32 [4, 16, 196608], P('grp', None, 'blk')
- residual: float32 [4, 16, 196608], P('grp', None, 'blk')
The draws below stay inside these ranges and needn't reach their ends.
Inputs may be any that keep to these rules, and one draw needn't show every extreme that they name: `dual_ops`: each subdomain's 1024 x 1024 block is symmetric positive definite. `prec_ops`: each subdomain's 1024 x 1024 block is symmetric positive definite. `signs`: every entry is 1 or -1; the lower face of each subdomain after the first of a group carries the negated signs of the upper face of the subdomain before it. `coarse_inverse`: symmetric positive definite.
All inputs are finite; a program needn't handle non-finite values.
Results may differ from the reference program's by a relative error of at most 0.003.
Values sent between devices are 32-bit elements; how exact they have to be, the bound alone decides.
A program may use at most 32 MiB of HBM per device.

```python
import math
import jax
import jax.numpy as jnp
from jax import lax

M = 1024
HALF = 512
NRHS = 16
NCG = 768
NC = 12
ITERS = 2
N_BLK = 192
N_GRP = 4


def symmetric_blocks(key, spread, low_diag, high_diag):

    def single(index):
        subkey = jax.random.fold_in(key, index)
        noise_key, diag_key = jax.random.split(subkey)
        noise = jax.random.truncated_normal(noise_key, -6.0, 6.0, (M, M), jnp.float32)
        mixed = (noise + noise.T) * (spread / math.sqrt(2.0 * M))
        diagonal = jnp.exp(jax.random.uniform(diag_key, (M,), jnp.float32, math.log(low_diag), math.log(high_diag)))
        return (mixed + jnp.diag(diagonal)).astype(jnp.bfloat16)
    blocks = lax.map(single, jnp.arange(N_GRP * N_BLK, dtype=jnp.int32))
    return blocks.reshape(N_GRP, N_BLK * M, M)


def draw_dual_ops(key, part):
    own_key = jax.random.fold_in(key, 11)
    return symmetric_blocks(own_key, 0.5, 1.5, 4.0)


def draw_prec_ops(key, part):
    own_key = jax.random.fold_in(key, 23)
    return symmetric_blocks(own_key, 0.3, 0.8, 2.5)


def draw_dual_rhs(key, part):
    own_key = jax.random.fold_in(key, 37)
    base_key = jax.random.fold_in(own_key, 0)
    columns = N_BLK * M
    position = jnp.arange(columns, dtype=jnp.float32) / (columns - 1)
    base = jax.random.truncated_normal(base_key, -4.0, 4.0, (N_GRP, NRHS, columns), jnp.float32)
    rising = jnp.exp(math.log(3.0) * position)
    return base * rising[None, None, :]


def draw_signs(key, part):
    own_key = jax.random.fold_in(key, 41)
    faces = 2 * N_BLK
    base = jax.random.randint(own_key, (N_GRP, faces, HALF), 0, 2, dtype=jnp.int32) * 2 - 1
    previous = jnp.roll(base, 1, axis=1)
    face_index = jnp.arange(faces, dtype=jnp.int32)[None, :, None]
    take_previous = (face_index % 2 == 0) & (face_index > 0)
    joined = jnp.where(take_previous, -previous, base)
    return joined.reshape(N_GRP, N_BLK * M).astype(jnp.int32)


def draw_coarse_inverse(key, part):
    own_key = jax.random.fold_in(key, 53)
    noise_key, diag_key = jax.random.split(own_key)
    noise = jax.random.truncated_normal(noise_key, -6.0, 6.0, (NCG, NCG), jnp.float32)
    mixed = (noise + noise.T) * (0.4 / math.sqrt(2.0 * NCG))
    diagonal = jnp.exp(jax.random.uniform(diag_key, (NCG,), jnp.float32, 0.0, math.log(3.0)))
    return mixed + jnp.diag(diagonal)


def touch_ends(array, key, least, high):
    longest = array.shape.index(max(array.shape))
    spots = []
    for shift in (0, 1):
        where = [jax.random.randint(jax.random.fold_in(key, axis), (), 0, length) for axis, length in enumerate(array.shape)]
        where[longest] = (where[longest] + shift) % array.shape[longest]
        spots.append(tuple(where))
    return array.at[spots[0]].set(least).at[spots[1]].set(high)


def levels(rng, extent, cuts, least, high):
    def one(axis_at, parts):
        steps = jax.random.uniform(jax.random.fold_in(jax.random.fold_in(rng, 6), axis_at), (parts,), jnp.float32, least / len(cuts), high / len(cuts))
        return jnp.repeat(jnp.exp(steps), extent[axis_at] // parts).reshape((-1,) + (1,) * (len(extent) - axis_at - 1))

    gain = one(*cuts[0])
    for cut in cuts[1:]:
        gain = gain * one(*cut)
    return gain


def gaussian(key, dims, scale, limit, shards=(), kind=jnp.bfloat16):
    array = jax.random.normal(key, dims, jnp.float32) * scale
    if len(shards) > 0:
        array = levels(key, dims, shards, -0.22, 0.18) * array
    return jnp.clip(array, min=-limit, max=limit).astype(kind)


def setup_inputs(seed: int = 0) -> dict:
    streams_of = jax.random.split(jax.random.key(seed), 8)
    return {
        "dual_rhs": draw_dual_rhs(jax.random.fold_in(streams_of[7], 71), 0),
        "dual_ops": draw_dual_ops(jax.random.fold_in(streams_of[7], 71), 0),
        "prec_ops": draw_prec_ops(jax.random.fold_in(streams_of[7], 71), 0),
        "corner_coupling": gaussian(streams_of[3], (N_GRP, N_BLK * 2 * NC, HALF), HALF ** -0.5, 0.25, ((0, 4), (1, 192))),
        "corner_map": touch_ends(jax.random.randint(streams_of[4], (N_GRP, N_BLK * 2 * NC), 0, NCG), jax.random.fold_in(streams_of[4], 1), 0, NCG - 1).astype(jnp.int32),
        "signs": draw_signs(jax.random.fold_in(streams_of[7], 71), 0),
        "coarse_inverse": draw_coarse_inverse(jax.random.fold_in(streams_of[7], 71), 0),
    }


def gram_solve(matrix, target):
    balanced = 0.5 * (matrix + matrix.T)
    factor = jnp.linalg.cholesky(balanced)
    middle = lax.linalg.triangular_solve(factor, target, left_side=True, lower=True)
    return lax.linalg.triangular_solve(factor, middle, left_side=True, lower=True, transpose_a=True)

def per_subdomain(operands):
    vector, block = operands
    return jnp.dot(vector.astype(jnp.float32), block.T.astype(jnp.float32), preferred_element_type=jnp.float32)

def reference(dual_rhs, dual_ops, prec_ops, corner_coupling, corner_map, signs, coarse_inverse):
    highest = lax.Precision.HIGHEST
    faces = 2 * N_BLK
    face_index = jnp.arange(faces, dtype=jnp.int32)
    live_face = ((face_index > 0) & (face_index < faces - 1)).astype(jnp.float32)
    even_face = face_index % 2 == 0
    face_sign = signs.reshape(N_GRP, faces, HALF).astype(jnp.float32) * live_face[None, :, None]
    couple = corner_coupling.reshape(N_GRP, faces, NC, HALF).astype(jnp.float32)
    corner_index = corner_map.reshape(N_GRP, faces, NC)
    dual_blocks = dual_ops.reshape(N_GRP * N_BLK, M, M)
    prec_blocks = prec_ops.reshape(N_GRP * N_BLK, M, M)

    def operate(values, blocks, coarse):
        signed_in = face_sign[:, None] * values
        rounded = signed_in.astype(jnp.bfloat16).reshape(N_GRP, NRHS, N_BLK, M)
        ordered = jnp.transpose(rounded, (0, 2, 1, 3)).reshape(N_GRP * N_BLK, NRHS, M)
        products = lax.map(per_subdomain, (ordered, blocks))
        local_out = jnp.transpose(products.reshape(N_GRP, N_BLK, NRHS, M), (0, 2, 1, 3)).reshape(N_GRP, NRHS, faces, HALF)
        if coarse:
            partial_value = jnp.einsum('grbh,gbch->gbcr', signed_in, couple, precision=highest)
            corner_sum = jax.ops.segment_sum(partial_value.reshape(-1, NRHS), corner_index.reshape(-1), num_segments=NCG)
            solved = jnp.dot(coarse_inverse, corner_sum, precision=highest)
            picked = solved[corner_index]
            local_out = local_out + jnp.einsum('gbcr,gbch->grbh', picked, couple, precision=highest)
        signed_out = face_sign[:, None] * local_out
        padding = jnp.zeros_like(signed_out[:, :, :1])
        from_left = jnp.concatenate([padding, signed_out[:, :, :-1]], axis=2)
        from_right = jnp.concatenate([signed_out[:, :, 1:], padding], axis=2)
        partner = jnp.where(even_face[None, None, :, None], from_left, from_right)
        return live_face[None, None, :, None] * (signed_out + partner)

    def inner(first, second):
        return jnp.einsum('grbh,gsbh->rs', first, second, precision=highest)

    def combine(weights, values):
        return jnp.einsum('rs,grbh->gsbh', weights, values, precision=highest)
    residual = live_face[None, None, :, None] * dual_rhs.reshape(N_GRP, NRHS, faces, HALF)
    multipliers = jnp.zeros_like(residual)
    precond = operate(residual, prec_blocks, False)
    gram_old = inner(residual, precond)
    direction = precond
    for iteration in range(ITERS):
        image_dir = operate(direction, dual_blocks, True)
        step_alpha = gram_solve(inner(direction, image_dir), gram_old)
        multipliers = multipliers + combine(step_alpha, direction)
        residual = residual - combine(step_alpha, image_dir)
        if iteration + 1 < ITERS:
            precond = operate(residual, prec_blocks, False)
            gram_new = inner(residual, precond)
            step_beta = gram_solve(gram_old, gram_new)
            direction = precond + combine(step_beta, direction)
            gram_old = gram_new
    return (multipliers.reshape(N_GRP, NRHS, N_BLK * M), residual.reshape(N_GRP, NRHS, N_BLK * M))
```

```python
import functools

import jax
import jax.numpy as jnp
from jax import lax
from jax.experimental import pallas as pl
from jax.experimental.pallas import tpu as pltpu
from jax.sharding import PartitionSpec as P

F32 = jnp.float32
BF16 = jnp.bfloat16
HIGHEST = lax.Precision.HIGHEST
LAST = (((1,), (1,)), ((), ()))
PLAIN = (((1,), (0,)), ((), ()))
FIRST = (((0,), (0,)), ((), ()))
NRHS = 16
HALF = 512
WIDTH = 2 * HALF
FACE_CORNERS = 12
CORNERS = 768
PAYLOAD = 1024


def split(value, terms):
    parts = []
    for _ in range(terms):
        part = value.astype(BF16)
        parts.append(part)
        value = value - part.astype(F32)
    return parts


def narrow_dot(value, exact, dims, terms=3):
    rows = value.shape[0]
    stacked = jnp.concatenate(split(value, terms), axis=0)
    out = lax.dot_general(stacked, exact, dims, preferred_element_type=F32)
    total = out[:rows]
    for term in range(1, terms):
        total = total + out[term * rows : (term + 1) * rows]
    return total


def full_dot(left, right, dims):
    return lax.dot_general(left, right, dims, precision=HIGHEST, preferred_element_type=F32)


def symmetric_part(matrix):
    return 0.5 * (matrix + matrix.T)


def spd_solve(matrix, target):
    size = matrix.shape[0]
    both = jnp.concatenate([matrix, target], axis=1)
    rows = lax.broadcasted_iota(jnp.int32, both.shape, 0)
    for k in range(size):
        column = jnp.broadcast_to(both[:, k : k + 1], both.shape)
        pivot_row = both[k : k + 1, :] / column[k : k + 1, :]
        both = jnp.where(rows == k, pivot_row, both - column * pivot_row)
    return both[:, size:]


def kernel(
    blk_count, grp_count, ny, nz,
    rhs_ref, prec_hbm, dual_hbm, couple_ref, map_ref, sign_ref, inverse_hbm,
    mult_ref, resid_ref,
    prec, dual, inverse, inverse_high, inverse_low,
    face_out, face_in, pieces, gathered, by_y, by_z, final,
    load_sem, face_send, face_recv,
    scatter_send, scatter_recv, y_send, y_recv, z_send, z_recv, final_send, final_recv,
):
    loads = [
        pltpu.make_async_copy(source, target, load_sem.at[index])
        for index, (source, target) in enumerate(
            ((prec_hbm, prec), (dual_hbm, dual), (inverse_hbm, inverse))
        )
    ]
    for load in loads:
        load.start()

    blk = lax.axis_index("blk")
    grp = lax.axis_index("grp")
    core = lax.rem(blk, 2)
    z = lax.rem(lax.div(blk, 2), nz)
    y = lax.div(blk, 2 * nz)
    spot = grp * 2 + core
    spots = 2 * grp_count
    lanes = PAYLOAD // spots

    def at(blk_index, grp_index):
        return {"blk": blk_index, "grp": grp_index}

    def spot_peer(step):
        other = lax.rem(spot + step, spots)
        return other, at(blk - core + lax.rem(other, 2), lax.div(other, 2))

    def y_peer(step):
        other = lax.rem(y + step, ny)
        return other, at(blk + (other - y) * (2 * nz), grp)

    def z_peer(step):
        other = lax.rem(z + step, nz)
        return other, at(blk + (other - z) * 2, grp)

    left = at(lax.rem(blk + blk_count - 1, blk_count), grp)
    right = at(lax.rem(blk + 1, blk_count), grp)

    barrier = pltpu.get_barrier_semaphore()
    greeted = [left, right]
    greeted += [spot_peer(step)[1] for step in range(1, spots)]
    greeted += [y_peer(step)[1] for step in range(1, ny)]
    greeted += [z_peer(step)[1] for step in range(1, nz)]
    for peer in greeted:
        pl.semaphore_signal(
            barrier, inc=1, device_id=peer, device_id_type=pl.DeviceIdType.MESH
        )

    def remote(source, target, send_sem, recv_sem, peer):
        return pltpu.make_async_remote_copy(
            src_ref=source,
            dst_ref=target,
            send_sem=send_sem,
            recv_sem=recv_sem,
            device_id=peer,
            device_id_type=pl.DeviceIdType.MESH,
        )

    def face_copies(turn):
        return (
            remote(
                face_out.at[turn, 0], face_in.at[turn, 1],
                face_send.at[turn, 0], face_recv.at[turn, 1], left,
            ),
            remote(
                face_out.at[turn, 1], face_in.at[turn, 0],
                face_send.at[turn, 1], face_recv.at[turn, 0], right,
            ),
        )

    def send_faces(turn, signed_out):
        face_out[turn, 0] = signed_out[:, :HALF]
        face_out[turn, 1] = signed_out[:, HALF:]
        for copy in face_copies(turn):
            copy.start()

    def take_faces(turn, signed_out):
        for copy in face_copies(turn):
            copy.wait_recv()
        partner = jnp.concatenate([face_in[turn, 0], face_in[turn, 1]], axis=1)
        return live * (signed_out + partner)

    def group_copies(peer_of, count, own, source_of, buffer, send_sem, recv_sem):
        copies = []
        for step in range(1, count):
            other, peer = peer_of(step)
            send = remote(source_of(other), buffer.at[own], send_sem.at[other], recv_sem.at[own], peer)
            recv = remote(source_of(other), buffer.at[other], send_sem.at[other], recv_sem.at[other], peer)
            copies.append((send, recv))
        return copies

    def start_all(copies):
        for send, _ in copies:
            send.start()

    def finish_all(copies):
        for _, recv in copies:
            recv.wait_recv()

    def drain_all(copies):
        for send, _ in copies:
            send.wait_send()

    def total_of(buffer, turn, count):
        total = buffer[turn, 0]
        for index in range(1, count):
            total = total + buffer[turn, index]
        return total

    def reduce_all(turn, payload, meanwhile):
        for index in range(spots):
            pieces[turn, index] = payload[:, index * lanes : (index + 1) * lanes]
        scatter = group_copies(
            spot_peer, spots, spot, lambda other: pieces.at[turn, other],
            gathered.at[turn], scatter_send.at[turn], scatter_recv.at[turn],
        )
        start_all(scatter)
        gathered[turn, spot] = pieces[turn, spot]
        between = meanwhile()
        finish_all(scatter)
        by_y[turn, y] = total_of(gathered, turn, spots)
        along_y = group_copies(
            y_peer, ny, y, lambda other: by_y.at[turn, y],
            by_y.at[turn], y_send.at[turn], y_recv.at[turn],
        )
        start_all(along_y)
        finish_all(along_y)
        by_z[turn, z] = total_of(by_y, turn, ny)
        along_z = group_copies(
            z_peer, nz, z, lambda other: by_z.at[turn, z],
            by_z.at[turn], z_send.at[turn], z_recv.at[turn],
        )
        start_all(along_z)
        finish_all(along_z)
        final[turn, spot] = total_of(by_z, turn, nz)
        spread = group_copies(
            spot_peer, spots, spot, lambda other: final.at[turn, spot],
            final.at[turn], final_send.at[turn], final_recv.at[turn],
        )
        start_all(spread)
        finish_all(spread)
        reduced = jnp.concatenate([final[turn, index] for index in range(spots)], axis=1)
        for copies in (scatter, along_y, along_z, spread):
            drain_all(copies)
        grams = [
            reduced[:, CORNERS + NRHS * index : CORNERS + NRHS * (index + 1)] for index in range(3)
        ]
        return reduced[:, :CORNERS], grams, between

    def pack(corner, grams):
        zeros = jnp.zeros((NRHS, PAYLOAD - CORNERS - NRHS * len(grams)), F32)
        return jnp.concatenate([corner, *grams, zeros], axis=1)

    lane = lax.broadcasted_iota(jnp.int32, (1, WIDTH), 1)
    lower_live = jnp.where(blk > 0, 1.0, 0.0).astype(F32)
    upper_live = jnp.where(blk < blk_count - 1, 1.0, 0.0).astype(F32)
    live = jnp.where(lane < HALF, lower_live, upper_live)
    face_sign = sign_ref[...].astype(F32) * live

    rows = 2 * FACE_CORNERS
    couple = couple_ref[0].astype(F32)
    couple_row = lax.broadcasted_iota(jnp.int32, couple.shape, 0)
    coupling = jnp.concatenate(
        [
            jnp.where(couple_row < FACE_CORNERS, couple, 0.0),
            jnp.where(couple_row >= FACE_CORNERS, couple, 0.0),
        ],
        axis=1,
    ).astype(BF16)
    diagonal = lax.broadcasted_iota(jnp.int32, (rows, rows), 0) == lax.broadcasted_iota(
        jnp.int32, (rows, rows), 1
    )
    map_row = jnp.broadcast_to(map_ref[...].astype(F32), (rows, rows))
    map_column = jnp.sum(jnp.where(diagonal, map_row, 0.0), axis=1, keepdims=True)
    corner_lane = lax.broadcasted_iota(jnp.int32, (rows, CORNERS), 1).astype(F32)
    onehot = jnp.where(map_column == corner_lane, 1.0, 0.0).astype(BF16)

    def local_product(values, blocks):
        return lax.dot_general(
            (face_sign * values).astype(BF16), blocks[...], PLAIN, preferred_element_type=F32
        )

    def corner_terms(values):
        partial = narrow_dot(face_sign * values, coupling, LAST)
        return narrow_dot(partial, onehot, PLAIN)

    def combine(weights, values):
        return full_dot(weights.T, values, PLAIN)

    residual = live * rhs_ref[0]
    loads[0].wait()
    signed_out = face_sign * local_product(residual, prec)
    pl.semaphore_wait(barrier, len(greeted))
    send_faces(0, signed_out)
    loads[1].wait()
    direction = take_faces(0, signed_out)
    corner = corner_terms(direction)
    image_local = local_product(direction, dual)
    payload = pack(
        corner,
        [
            full_dot(residual, direction, LAST),
            2.0 * full_dot(face_sign * direction, image_local, LAST),
        ],
    )

    def prepare():
        loads[2].wait()
        high, middle, low = split(inverse[...], 3)
        inverse_high[...] = high
        inverse_low[...] = middle
        picked = lax.dot_general(onehot, high, PLAIN, preferred_element_type=F32)
        picked = picked + lax.dot_general(onehot, middle, PLAIN, preferred_element_type=F32)
        return picked + lax.dot_general(onehot, low, PLAIN, preferred_element_type=F32)

    corner_old, (gram_old, curve_local, _), inverse_rows = reduce_all(0, payload, prepare)

    def solve_corners(values):
        high, low = split(values, 2)
        both = lax.dot_general(
            jnp.concatenate([high, low], axis=0), inverse_high[...], PLAIN,
            preferred_element_type=F32,
        )
        cross = lax.dot_general(high, inverse_low[...], PLAIN, preferred_element_type=F32)
        return both[:NRHS] + (both[NRHS:] + cross)

    picked_old = full_dot(corner_old, inverse_rows, LAST)
    signed_out = face_sign * (image_local + narrow_dot(picked_old, coupling, PLAIN))
    send_faces(1, signed_out)
    solved_old = solve_corners(corner_old)
    curve_old = curve_local + 2.0 * full_dot(corner_old, solved_old, LAST)
    curve_old = symmetric_part(curve_old)
    alpha = spd_solve(curve_old, gram_old)
    image_dir = take_faces(1, signed_out)
    residual = residual - combine(alpha, image_dir)
    signed_out = face_sign * local_product(residual, prec)
    send_faces(2, signed_out)
    multipliers = combine(alpha, direction)
    precond = take_faces(2, signed_out)
    corner = corner_terms(precond)
    precond_local = local_product(precond, dual)
    signed_precond = face_sign * precond
    payload = pack(
        corner,
        [
            full_dot(residual, precond, LAST),
            2.0 * full_dot(signed_precond, precond_local, LAST),
            2.0 * full_dot(signed_precond, image_local, LAST),
        ],
    )

    def invert():
        unit = lax.broadcasted_iota(jnp.int32, (NRHS, NRHS), 0) == lax.broadcasted_iota(
            jnp.int32, (NRHS, NRHS), 1
        )
        return spd_solve(symmetric_part(gram_old), jnp.where(unit, 1.0, 0.0).astype(F32))

    corner_new, (gram_new, curve_new, cross), gram_inverse = reduce_all(1, payload, invert)
    beta = full_dot(gram_inverse, gram_new, PLAIN)
    direction = precond + combine(beta, direction)
    picked = full_dot(corner_new, inverse_rows, LAST) + combine(beta, picked_old)
    signed_out = face_sign * (
        local_product(direction, dual) + narrow_dot(picked, coupling, PLAIN)
    )
    send_faces(3, signed_out)
    solved_new = solve_corners(corner_new)
    curve_new = curve_new + 2.0 * full_dot(corner_new, solved_new, LAST)
    cross = cross + 2.0 * full_dot(corner_new, solved_old, LAST)
    mixed = full_dot(cross, beta, PLAIN)
    quadratic = full_dot(beta.T, full_dot(curve_old, beta, PLAIN), PLAIN)
    curve = symmetric_part(curve_new + 2.0 * mixed + quadratic)
    alpha = spd_solve(curve, gram_new)
    mult_ref[0] = multipliers + combine(alpha, direction)
    image_dir = take_faces(3, signed_out)
    resid_ref[0] = residual - combine(alpha, image_dir)
    for turn in range(4):
        for copy in face_copies(turn):
            copy.wait_send()


def extents(blk_count):
    return {192: (8, 12), 8: (2, 2)}[blk_count]


def solution(mesh):
    blk_count, grp_count = mesh.shape["blk"], mesh.shape["grp"]
    ny, nz = extents(blk_count)
    spots = 2 * grp_count
    piece = (NRHS, PAYLOAD // spots)
    dma = pltpu.SemaphoreType.DMA
    in_vmem = pl.BlockSpec(memory_space=pltpu.VMEM)
    in_place = pl.BlockSpec(memory_space=pl.ANY)

    def local(dual_rhs, dual_ops, prec_ops, corner_coupling, corner_map, signs, coarse_inverse):
        result = jax.ShapeDtypeStruct((1, NRHS, WIDTH), F32)
        return pl.pallas_call(
            functools.partial(kernel, blk_count, grp_count, ny, nz),
            out_shape=(result, result),
            in_specs=[in_vmem, in_place, in_place, in_vmem, in_vmem, in_vmem, in_place],
            out_specs=(in_vmem, in_vmem),
            scratch_shapes=[
                pltpu.VMEM((WIDTH, WIDTH), BF16),
                pltpu.VMEM((WIDTH, WIDTH), BF16),
                pltpu.VMEM((CORNERS, CORNERS), F32),
                pltpu.VMEM((CORNERS, CORNERS), BF16),
                pltpu.VMEM((CORNERS, CORNERS), BF16),
                pltpu.VMEM((4, 2, NRHS, HALF), F32),
                pltpu.VMEM((4, 2, NRHS, HALF), F32),
                pltpu.VMEM((2, spots, *piece), F32),
                pltpu.VMEM((2, spots, *piece), F32),
                pltpu.VMEM((2, ny, *piece), F32),
                pltpu.VMEM((2, nz, *piece), F32),
                pltpu.VMEM((2, spots, *piece), F32),
                dma((3,)),
                dma((4, 2)),
                dma((4, 2)),
                dma((2, spots)),
                dma((2, spots)),
                dma((2, ny)),
                dma((2, ny)),
                dma((2, nz)),
                dma((2, nz)),
                dma((2, spots)),
                dma((2, spots)),
            ],
            compiler_params=pltpu.CompilerParams(
                collective_id=0, has_side_effects=True, vmem_limit_bytes=48 * 1024 * 1024
            ),
            name="block_conjugate_gradients",
        )(
            dual_rhs, prec_ops.reshape(WIDTH, WIDTH), dual_ops.reshape(WIDTH, WIDTH),
            corner_coupling, corner_map, signs, coarse_inverse,
        )

    in_specs = (
        P("grp", None, "blk"),
        P("grp", "blk", None),
        P("grp", "blk", None),
        P("grp", "blk", None),
        P("grp", "blk"),
        P("grp", "blk"),
        P(),
    )
    out_specs = (P("grp", None, "blk"), P("grp", None, "blk"))
    return jax.shard_map(local, mesh=mesh, in_specs=in_specs, out_specs=out_specs, check_vma=False)
```

```python
import functools

import jax
import jax.numpy as jnp
from jax import lax
from jax.experimental import pallas as pl
from jax.experimental.pallas import tpu as pltpu
from jax.sharding import PartitionSpec as P

F32 = jnp.float32
BF16 = jnp.bfloat16
HIGHEST = lax.Precision.HIGHEST
LAST = (((1,), (1,)), ((), ()))
PLAIN = (((1,), (0,)), ((), ()))
FIRST = (((0,), (0,)), ((), ()))
NRHS = 16
HALF = 512
WIDTH = 2 * HALF
FACE_CORNERS = 12
CORNERS = 768
PAYLOAD = 1024
BLOCKS = 4


def split(value, terms):
    parts = []
    for _ in range(terms):
        part = value.astype(BF16)
        parts.append(part)
        value = value - part.astype(F32)
    return parts


def narrow_dot(value, exact, dims, terms=3):
    rows = value.shape[0]
    stacked = jnp.concatenate(split(value, terms), axis=0)
    out = lax.dot_general(stacked, exact, dims, preferred_element_type=F32)
    total = out[:rows]
    for term in range(1, terms):
        total = total + out[term * rows : (term + 1) * rows]
    return total


def full_dot(left, right, dims):
    return lax.dot_general(left, right, dims, precision=HIGHEST, preferred_element_type=F32)


def symmetric_part(matrix):
    return 0.5 * (matrix + matrix.T)


def spd_solve(matrix, target):
    size = matrix.shape[0]
    both = jnp.concatenate([matrix, target], axis=1)
    rows = lax.broadcasted_iota(jnp.int32, both.shape, 0)
    for k in range(size):
        column = jnp.broadcast_to(both[:, k : k + 1], both.shape)
        pivot_row = both[k : k + 1, :] / column[k : k + 1, :]
        both = jnp.where(rows == k, pivot_row, both - column * pivot_row)
    return both[:, size:]


def kernel(
    blk_count, grp_count, ny, nz,
    rhs_hbm, prec_hbm, dual_hbm, couple_hbm, map_hbm, sign_hbm, inverse_hbm,
    mult_ref, resid_ref,
    rhs, prec, dual, couple, corner_map, signs, inverse, inverse_high, inverse_low,
    face_out, face_in, pieces, gathered, by_y, by_z, final, gram_spot, gram_y, gram_z,
    load_sem, prec_sem, face_send, face_recv,
    scatter_send, scatter_recv, y_send, y_recv, z_send, z_recv, final_send, final_recv,
    gram_send, gram_recv, gram_y_send, gram_y_recv, gram_z_send, gram_z_recv,
):
    small_loads = [
        pltpu.make_async_copy(source, target, load_sem.at[index])
        for index, (source, target) in enumerate(
            ((couple_hbm, couple), (map_hbm, corner_map), (rhs_hbm, rhs), (sign_hbm, signs))
        )
    ]
    block_rows = WIDTH // BLOCKS
    prec_loads = [
        pltpu.make_async_copy(
            prec_hbm.at[pl.ds(index * block_rows, block_rows)],
            prec.at[pl.ds(index * block_rows, block_rows)],
            prec_sem.at[index],
        )
        for index in range(BLOCKS)
    ]
    late_loads = [
        pltpu.make_async_copy(dual_hbm, dual, load_sem.at[4]),
        pltpu.make_async_copy(inverse_hbm, inverse, load_sem.at[5]),
    ]
    for load in small_loads + prec_loads:
        load.start()

    blk = lax.axis_index("blk")
    grp = lax.axis_index("grp")
    core = lax.rem(blk, 2)
    z = lax.rem(lax.div(blk, 2), nz)
    y = lax.div(blk, 2 * nz)
    spot = grp * 2 + core
    spots = 2 * grp_count
    lanes = PAYLOAD // spots

    def at(blk_index, grp_index):
        return {"blk": blk_index, "grp": grp_index}

    def spot_peer(step):
        other = lax.rem(spot + step, spots)
        return other, at(blk - core + lax.rem(other, 2), lax.div(other, 2))

    def y_peer(step):
        other = lax.rem(y + step, ny)
        return other, at(blk + (other - y) * (2 * nz), grp)

    def z_peer(step):
        other = lax.rem(z + step, nz)
        return other, at(blk + (other - z) * 2, grp)

    left = at(lax.rem(blk + blk_count - 1, blk_count), grp)
    right = at(lax.rem(blk + 1, blk_count), grp)

    barrier = pltpu.get_barrier_semaphore()
    greeted = [z_peer(step)[1] for step in range(1, nz)]
    greeted += [y_peer(step)[1] for step in range(1, ny)]
    greeted += [spot_peer(step)[1] for step in range(1, spots)]
    greeted += [left, right]
    for peer in greeted:
        pl.semaphore_signal(
            barrier, inc=1, device_id=peer, device_id_type=pl.DeviceIdType.MESH
        )

    def remote(source, target, send_sem, recv_sem, peer):
        return pltpu.make_async_remote_copy(
            src_ref=source,
            dst_ref=target,
            send_sem=send_sem,
            recv_sem=recv_sem,
            device_id=peer,
            device_id_type=pl.DeviceIdType.MESH,
        )

    def face_copies(turn):
        return (
            remote(
                face_out.at[turn, 0], face_in.at[turn, 1],
                face_send.at[turn, 0], face_recv.at[turn, 1], left,
            ),
            remote(
                face_out.at[turn, 1], face_in.at[turn, 0],
                face_send.at[turn, 1], face_recv.at[turn, 0], right,
            ),
        )

    def send_faces(turn, lower, upper):
        face_out[turn, 0] = lower
        face_out[turn, 1] = upper
        for copy in face_copies(turn):
            copy.start()

    def send_signed(turn, signed_out):
        send_faces(turn, signed_out[:, :HALF], signed_out[:, HALF:])

    def wait_faces(turn):
        for copy in face_copies(turn):
            copy.wait_recv()

    def take_faces(turn, signed_out):
        wait_faces(turn)
        partner = jnp.concatenate([face_in[turn, 0], face_in[turn, 1]], axis=1)
        return live * (signed_out + partner)

    drains = []

    def exchange(peer_of, count, own, source_of, buffer, send_sem, recv_sem):
        arrivals = []
        for step in range(1, count):
            other, peer = peer_of(step)
            send = remote(source_of(other), buffer.at[own], send_sem.at[other], recv_sem.at[own], peer)
            send.start()
            drains.append(send)
            arrivals.append(
                remote(source_of(other), buffer.at[other], send_sem.at[other], recv_sem.at[other], peer)
            )

        def arrive():
            for copy in arrivals:
                copy.wait_recv()

        return arrive

    def spread(peer_of, count, own, buffer, send_sem, recv_sem, value):
        buffer[own] = value
        return exchange(
            peer_of, count, own, lambda other: buffer.at[own], buffer, send_sem, recv_sem
        )

    def total_of(buffer, count):
        terms = [buffer[index] for index in range(count)]
        while len(terms) > 1:
            terms = [sum(terms[index : index + 2]) for index in range(0, len(terms), 2)]
        return terms[0]

    def padded(face_couple, face_map):
        size = NRHS - FACE_CORNERS
        block = jnp.concatenate([face_couple, jnp.zeros((size, HALF), F32)], axis=0)
        row = jnp.concatenate([face_map, jnp.zeros((1, HALF - FACE_CORNERS), F32)], axis=1)
        return jnp.where(block_row == FACE_CORNERS, row, block)

    def coupling_of(block):
        return jnp.where(block_row < FACE_CORNERS, block, 0.0)

    def onehot_of(block):
        row = jnp.broadcast_to(block[FACE_CORNERS : FACE_CORNERS + 1, :128], (NRHS, 128))
        column = jnp.sum(jnp.where(diagonal, row, 0.0), axis=1, keepdims=True)
        hit = jnp.logical_and(column == corner_lane, corner_row < FACE_CORNERS)
        return jnp.where(hit, 1.0, 0.0)

    block_row = lax.broadcasted_iota(jnp.int32, (NRHS, HALF), 0)
    corner_row = lax.broadcasted_iota(jnp.int32, (NRHS, CORNERS), 0)
    corner_lane = lax.broadcasted_iota(jnp.int32, (NRHS, CORNERS), 1).astype(F32)
    diagonal = lax.broadcasted_iota(jnp.int32, (NRHS, 128), 0) == lax.broadcasted_iota(
        jnp.int32, (NRHS, 128), 1
    )
    lane = lax.broadcasted_iota(jnp.int32, (1, WIDTH), 1)
    lower_live = jnp.where(blk > 0, 1.0, 0.0).astype(F32)
    upper_live = jnp.where(blk < blk_count - 1, 1.0, 0.0).astype(F32)
    live = jnp.where(lane < HALF, lower_live, upper_live)

    small_loads[0].wait()
    small_loads[1].wait()
    couple_all = couple[0].astype(F32)
    map_all = corner_map[...].astype(F32)
    own_lower = padded(couple_all[:FACE_CORNERS], map_all[:, :FACE_CORNERS])
    own_upper = padded(couple_all[FACE_CORNERS:], map_all[:, FACE_CORNERS:])
    pl.semaphore_wait(barrier, len(greeted))
    send_faces(0, own_lower, own_upper)

    small_loads[2].wait()
    small_loads[3].wait()
    face_sign = signs[...].astype(F32) * live
    residual = live * rhs[0]

    def prec_product(values, wait):
        rounded = (face_sign * values).astype(BF16)
        total = None
        for index in range(BLOCKS):
            if wait:
                prec_loads[index].wait()
            span = slice(index * block_rows, (index + 1) * block_rows)
            part = lax.dot_general(
                rounded[:, span], prec[span, :], PLAIN, preferred_element_type=F32
            )
            total = part if total is None else total + part
        return total

    local_out = prec_product(residual, True)
    for load in late_loads:
        load.start()
    send_signed(1, face_sign * local_out)

    wait_faces(0)
    across_lower = face_in[0, 0]
    across_upper = face_in[0, 1]
    zeros = jnp.zeros((NRHS, HALF), F32)
    coupling = jnp.concatenate(
        [
            jnp.concatenate([coupling_of(own_lower), zeros], axis=1),
            jnp.concatenate([zeros, coupling_of(own_upper)], axis=1),
            jnp.concatenate([-coupling_of(across_lower), zeros], axis=1),
            jnp.concatenate([zeros, -coupling_of(across_upper)], axis=1),
        ],
        axis=0,
    ).astype(BF16)
    onehot = jnp.concatenate(
        [onehot_of(block) for block in (own_lower, own_upper, across_lower, across_upper)], axis=0
    ).astype(BF16)

    def combine(weights, values):
        return full_dot(weights.T, values, PLAIN)

    def reduce_all(turn, local_out, meanwhile):
        signed_out = face_sign * local_out
        face_turn = 1 + 3 * turn
        partial = narrow_dot(live * local_out, coupling, LAST)
        corner = narrow_dot(partial, onehot, PLAIN)
        for index in range(spots):
            first = index * lanes
            pieces[turn, index] = (
                corner[:, first : first + lanes]
                if first < CORNERS
                else jnp.zeros((NRHS, lanes), F32)
            )
        scattered = exchange(
            spot_peer, spots, spot, lambda other: pieces.at[turn, other],
            gathered.at[turn], scatter_send.at[turn], scatter_recv.at[turn],
        )
        gathered[turn, spot] = pieces[turn, spot]
        precond = take_faces(face_turn, signed_out)
        signed_in = face_sign * precond
        if turn == 0:
            late_loads[0].wait()
        high, low = split(signed_in, 2)
        both = lax.dot_general(
            jnp.concatenate([high, low], axis=0), dual[...], PLAIN, preferred_element_type=F32
        )
        product, correction = both[:NRHS], both[NRHS:]
        scattered()
        along_y = spread(
            y_peer, ny, y, by_y.at[turn], y_send.at[turn], y_recv.at[turn],
            total_of(gathered.at[turn], spots),
        )
        grams = [
            full_dot(residual, precond, LAST),
            2.0 * full_dot(signed_in, product, LAST),
            2.0 * full_dot(signed_in, product if turn == 0 else product_old, LAST),
            jnp.zeros((NRHS, NRHS), F32),
        ]
        wide = jnp.concatenate(grams, axis=1)
        packed = jnp.concatenate([wide[:8], wide[8:]], axis=1)
        gram_at_spot = spread(
            spot_peer, spots, spot, gram_spot.at[turn], gram_send.at[turn], gram_recv.at[turn], packed
        )
        send_signed(face_turn + 1, face_sign * product)
        send_signed(face_turn + 2, face_sign * correction)
        along_y()
        along_z = spread(
            z_peer, nz, z, by_z.at[turn], z_send.at[turn], z_recv.at[turn],
            total_of(by_y.at[turn], ny),
        )
        gram_at_spot()
        gram_along_y = spread(
            y_peer, ny, y, gram_y.at[turn], gram_y_send.at[turn], gram_y_recv.at[turn],
            total_of(gram_spot.at[turn], spots),
        )
        between = meanwhile()
        gram_along_y()
        gram_along_z = spread(
            z_peer, nz, z, gram_z.at[turn], gram_z_send.at[turn], gram_z_recv.at[turn],
            total_of(gram_y.at[turn], ny),
        )
        along_z()
        gathered_back = spread(
            spot_peer, spots, spot, final.at[turn], final_send.at[turn], final_recv.at[turn],
            total_of(by_z.at[turn], nz),
        )
        image = take_faces(face_turn + 1, face_sign * product)
        correction = take_faces(face_turn + 2, face_sign * correction)
        gathered_back()
        corner = jnp.concatenate([final[turn, index] for index in range(spots)], axis=1)

        def take_grams():
            gram_along_z()
            total = total_of(gram_z.at[turn], nz)
            wide = jnp.concatenate([total[:, :64], total[:, 64:]], axis=0)
            return [wide[:, index * NRHS : (index + 1) * NRHS] for index in range(3)]

        return precond, product, image, correction, corner[:, :CORNERS], take_grams, between

    def prepare():
        late_loads[1].wait()
        high, middle, low = split(inverse[...], 3)
        inverse_high[...] = high
        inverse_low[...] = middle
        picked = lax.dot_general(onehot, high, PLAIN, preferred_element_type=F32)
        picked = picked + lax.dot_general(onehot, middle, PLAIN, preferred_element_type=F32)
        return picked + lax.dot_general(onehot, low, PLAIN, preferred_element_type=F32)

    def solve_corners(values):
        high, low = split(values, 2)
        both = lax.dot_general(
            jnp.concatenate([high, low], axis=0), inverse_high[...], PLAIN,
            preferred_element_type=F32,
        )
        cross = lax.dot_general(high, inverse_low[...], PLAIN, preferred_element_type=F32)
        return both[:NRHS] + (both[NRHS:] + cross)

    def coarse_image(corner):
        picked = full_dot(corner, inverse_rows, LAST)
        return face_sign * narrow_dot(picked, coupling, PLAIN)

    product_old = None
    direction, product_old, image_old, correction_old, corner_old, take_grams, inverse_rows = (
        reduce_all(0, local_out, prepare)
    )
    solved_old = solve_corners(corner_old)
    curve_coarse = 2.0 * full_dot(corner_old, solved_old, LAST)
    image_old = image_old + coarse_image(corner_old)
    gram_old, curve_old, _ = take_grams()
    curve_old = symmetric_part(curve_old + curve_coarse)
    alpha_old = spd_solve(curve_old, gram_old)
    residual = residual - combine(alpha_old, image_old)
    local_out = prec_product(residual, False)
    send_signed(4, face_sign * local_out)
    image_old = image_old + correction_old

    def invert():
        unit = lax.broadcasted_iota(jnp.int32, (NRHS, NRHS), 0) == lax.broadcasted_iota(
            jnp.int32, (NRHS, NRHS), 1
        )
        return spd_solve(symmetric_part(gram_old), jnp.where(unit, 1.0, 0.0).astype(F32))

    precond, _, image, correction, corner_new, take_grams, gram_inverse = reduce_all(
        1, local_out, invert
    )
    solved_new = solve_corners(corner_new)
    curve_coarse = 2.0 * full_dot(corner_new, solved_new, LAST)
    cross_coarse = 2.0 * full_dot(corner_new, solved_old, LAST)
    image = image + correction + coarse_image(corner_new)
    gram_new, curve_new, cross = take_grams()
    beta = full_dot(gram_inverse, gram_new, PLAIN)
    mixed = full_dot(cross + cross_coarse, beta, PLAIN)
    quadratic = full_dot(beta.T, full_dot(curve_old, beta, PLAIN), PLAIN)
    curve = symmetric_part(curve_new + curve_coarse + 2.0 * mixed + quadratic)
    alpha = spd_solve(curve, gram_new)
    through = full_dot(beta, alpha, PLAIN)
    mult_ref[0] = combine(
        jnp.concatenate([alpha_old + through, alpha], axis=0),
        jnp.concatenate([direction, precond], axis=0),
    )
    resid_ref[0] = residual - combine(
        jnp.concatenate([through, alpha], axis=0), jnp.concatenate([image_old, image], axis=0)
    )
    for copy in drains:
        copy.wait_send()
    for turn in range(7):
        for copy in face_copies(turn):
            copy.wait_send()


def extents(blk_count):
    return {192: (8, 12), 8: (2, 2)}[blk_count]


def solution(mesh):
    blk_count, grp_count = mesh.shape["blk"], mesh.shape["grp"]
    ny, nz = extents(blk_count)
    spots = 2 * grp_count
    piece = (NRHS, PAYLOAD // spots)
    dma = pltpu.SemaphoreType.DMA
    in_vmem = pl.BlockSpec(memory_space=pltpu.VMEM)
    in_place = pl.BlockSpec(memory_space=pl.ANY)

    def local(dual_rhs, dual_ops, prec_ops, corner_coupling, corner_map, signs, coarse_inverse):
        result = jax.ShapeDtypeStruct((1, NRHS, WIDTH), F32)
        return pl.pallas_call(
            functools.partial(kernel, blk_count, grp_count, ny, nz),
            out_shape=(result, result),
            in_specs=[in_place] * 7,
            out_specs=(in_vmem, in_vmem),
            scratch_shapes=[
                pltpu.VMEM((1, NRHS, WIDTH), F32),
                pltpu.VMEM((WIDTH, WIDTH), BF16),
                pltpu.VMEM((WIDTH, WIDTH), BF16),
                pltpu.VMEM((1, 2 * FACE_CORNERS, HALF), BF16),
                pltpu.VMEM((1, 2 * FACE_CORNERS), jnp.int32),
                pltpu.VMEM((1, WIDTH), jnp.int32),
                pltpu.VMEM((CORNERS, CORNERS), F32),
                pltpu.VMEM((CORNERS, CORNERS), BF16),
                pltpu.VMEM((CORNERS, CORNERS), BF16),
                pltpu.VMEM((7, 2, NRHS, HALF), F32),
                pltpu.VMEM((7, 2, NRHS, HALF), F32),
                pltpu.VMEM((2, spots, *piece), F32),
                pltpu.VMEM((2, spots, *piece), F32),
                pltpu.VMEM((2, ny, *piece), F32),
                pltpu.VMEM((2, nz, *piece), F32),
                pltpu.VMEM((2, spots, *piece), F32),
                pltpu.VMEM((2, spots, 8, 128), F32),
                pltpu.VMEM((2, ny, 8, 128), F32),
                pltpu.VMEM((2, nz, 8, 128), F32),
                dma((6,)),
                dma((BLOCKS,)),
                dma((7, 2)),
                dma((7, 2)),
                *[dma((2, count)) for count in (spots, ny, nz, spots, spots, ny, nz) for _ in range(2)],
            ],
            compiler_params=pltpu.CompilerParams(
                collective_id=0, has_side_effects=True, vmem_limit_bytes=67043328
            ),
            name="block_conjugate_gradients",
        )(
            dual_rhs, prec_ops.reshape(WIDTH, WIDTH), dual_ops.reshape(WIDTH, WIDTH),
            corner_coupling, corner_map, signs, coarse_inverse,
        )

    in_specs = (
        P("grp", None, "blk"),
        P("grp", "blk", None),
        P("grp", "blk", None),
        P("grp", "blk", None),
        P("grp", "blk"),
        P("grp", "blk"),
        P(),
    )
    out_specs = (P("grp", None, "blk"), P("grp", None, "blk"))
    return jax.shard_map(local, mesh=mesh, in_specs=in_specs, out_specs=out_specs, check_vma=False)
```

```python
import functools

import jax
import jax.numpy as jnp
from jax import lax
from jax.experimental import pallas as pl
from jax.experimental.pallas import tpu as pltpu
from jax.sharding import PartitionSpec as P

F32 = jnp.float32
BF16 = jnp.bfloat16
HIGHEST = lax.Precision.HIGHEST
LAST = (((1,), (1,)), ((), ()))
PLAIN = (((1,), (0,)), ((), ()))
FIRST = (((0,), (0,)), ((), ()))
NRHS = 16
HALF = 512
WIDTH = 2 * HALF
FACE_CORNERS = 12
CORNERS = 768
BLOCKS = 4
TURNS = 6
CORRECTION = 5


def split(value, terms):
    parts = []
    for _ in range(terms):
        part = value.astype(BF16)
        parts.append(part)
        value = value - part.astype(F32)
    return parts


def narrow_dot(value, exact, dims, terms=3):
    rows = value.shape[0]
    stacked = jnp.concatenate(split(value, terms), axis=0)
    out = lax.dot_general(stacked, exact, dims, preferred_element_type=F32)
    total = out[:rows]
    for term in range(1, terms):
        total = total + out[term * rows : (term + 1) * rows]
    return total


def full_dot(left, right, dims):
    return lax.dot_general(left, right, dims, precision=HIGHEST, preferred_element_type=F32)


def to_pieces(corner, spots):
    tiles = [
        corner[8 * (index % 2) : 8 * (index % 2) + 8, 128 * (index // 2) : 128 * (index // 2) + 128]
        for index in range(NRHS * CORNERS // 1024)
    ]
    share = len(tiles) * 8 // spots
    if share % 8 == 0:
        many = share // 8
        return [
            jnp.concatenate(tiles[index * many : (index + 1) * many], axis=0)
            for index in range(spots)
        ]
    pieces = []
    for index in range(0, len(tiles), 3):
        first, middle, last = tiles[index : index + 3]
        pieces.append(jnp.concatenate([first, middle[:4]], axis=0))
        pieces.append(jnp.concatenate([last, middle[4:]], axis=0))
    return pieces


def from_pieces(pieces):
    tiles = []
    if pieces[0].shape[0] % 8 == 0:
        for piece in pieces:
            tiles += [piece[index : index + 8] for index in range(0, piece.shape[0], 8)]
    else:
        for first, last in zip(pieces[::2], pieces[1::2]):
            tiles += [first[:8], jnp.concatenate([first[8:], last[8:]], axis=0), last[:8]]
    columns = [
        jnp.concatenate(tiles[index : index + 2], axis=0) for index in range(0, len(tiles), 2)
    ]
    return jnp.concatenate(columns, axis=1)


def symmetric_part(matrix):
    return 0.5 * (matrix + matrix.T)


def spd_solve(matrix, target):
    size = matrix.shape[0]
    both = jnp.concatenate([matrix, target], axis=1)
    rows = lax.broadcasted_iota(jnp.int32, both.shape, 0)
    for k in range(size):
        column = jnp.broadcast_to(both[:, k : k + 1], both.shape)
        pivot_row = both[k : k + 1, :] / column[k : k + 1, :]
        both = jnp.where(rows == k, pivot_row, both - column * pivot_row)
    return both[:, size:]


def kernel(
    blk_count, grp_count, ny, nz,
    rhs_hbm, prec_hbm, dual_hbm, couple_hbm, map_hbm, sign_hbm, inverse_hbm,
    out_ref,
    rhs, prec, dual, couple, corner_map, signs, inverse, inverse_high, inverse_low,
    face_out, face_in, pieces, gathered, by_y, by_z, final, gram_spot, gram_y, gram_z,
    load_sem, prec_sem, face_send, face_recv,
    scatter_send, scatter_recv, y_send, y_recv, z_send, z_recv, final_send, final_recv,
    gram_send, gram_recv, gram_y_send, gram_y_recv, gram_z_send, gram_z_recv,
):
    small_loads = [
        pltpu.make_async_copy(source, target, load_sem.at[index])
        for index, (source, target) in enumerate(
            ((couple_hbm, couple), (map_hbm, corner_map), (rhs_hbm, rhs), (sign_hbm, signs))
        )
    ]
    block_rows = WIDTH // BLOCKS
    prec_loads = [
        pltpu.make_async_copy(
            prec_hbm.at[pl.ds(index * block_rows, block_rows)],
            prec.at[pl.ds(index * block_rows, block_rows)],
            prec_sem.at[index],
        )
        for index in range(BLOCKS)
    ]
    late_loads = [
        pltpu.make_async_copy(dual_hbm, dual, load_sem.at[4]),
        pltpu.make_async_copy(inverse_hbm, inverse, load_sem.at[5]),
    ]
    for load in small_loads + prec_loads:
        load.start()

    blk = lax.axis_index("blk")
    grp = lax.axis_index("grp")
    core = lax.rem(blk, 2)
    z = lax.rem(lax.div(blk, 2), nz)
    y = lax.div(blk, 2 * nz)
    spot = grp * 2 + core
    spots = 2 * grp_count

    def at(blk_index, grp_index):
        return {"blk": blk_index, "grp": grp_index}

    def spot_peer(step):
        other = lax.rem(spot + step, spots)
        return other, at(blk - core + lax.rem(other, 2), lax.div(other, 2))

    def y_peer(step):
        other = lax.rem(y + step, ny)
        return other, at(blk + (other - y) * (2 * nz), grp)

    def z_peer(step):
        other = lax.rem(z + step, nz)
        return other, at(blk + (other - z) * 2, grp)

    left = at(lax.rem(blk + blk_count - 1, blk_count), grp)
    right = at(lax.rem(blk + 1, blk_count), grp)

    barrier = pltpu.get_barrier_semaphore()
    greeted = [z_peer(step)[1] for step in range(1, nz)]
    greeted += [y_peer(step)[1] for step in range(1, ny)]
    greeted += [spot_peer(step)[1] for step in range(1, spots)]
    greeted += [left, right]
    for peer in greeted:
        pl.semaphore_signal(
            barrier, inc=1, device_id=peer, device_id_type=pl.DeviceIdType.MESH
        )

    def remote(source, target, send_sem, recv_sem, peer):
        return pltpu.make_async_remote_copy(
            src_ref=source,
            dst_ref=target,
            send_sem=send_sem,
            recv_sem=recv_sem,
            device_id=peer,
            device_id_type=pl.DeviceIdType.MESH,
        )

    def face_copies(turn):
        return (
            remote(
                face_out.at[turn, 0], face_in.at[turn, 1],
                face_send.at[turn, 0], face_recv.at[turn, 1], left,
            ),
            remote(
                face_out.at[turn, 1], face_in.at[turn, 0],
                face_send.at[turn, 1], face_recv.at[turn, 0], right,
            ),
        )

    def send_faces(turn, lower, upper):
        face_out[turn, 0] = lower
        face_out[turn, 1] = upper
        for copy in face_copies(turn):
            copy.start()

    def send_signed(turn, signed_out):
        send_faces(turn, signed_out[:, :HALF], signed_out[:, HALF:])

    def wait_faces(turn):
        for copy in face_copies(turn):
            copy.wait_recv()

    def take_faces(turn, signed_out):
        wait_faces(turn)
        partner = jnp.concatenate([face_in[turn, 0], face_in[turn, 1]], axis=1)
        return live * (signed_out + partner)

    drains = []

    def exchange(peer_of, count, own, source_of, buffer, send_sem, recv_sem):
        arrivals = []
        for step in range(1, count):
            other, peer = peer_of(step)
            send = remote(source_of(other), buffer.at[own], send_sem.at[other], recv_sem.at[own], peer)
            send.start()
            drains.append(send)
            arrivals.append(
                remote(source_of(other), buffer.at[other], send_sem.at[other], recv_sem.at[other], peer)
            )

        def arrive():
            for copy in arrivals:
                copy.wait_recv()

        return arrive

    def spread(peer_of, count, own, buffer, send_sem, recv_sem, value):
        buffer[own] = value
        return exchange(
            peer_of, count, own, lambda other: buffer.at[own], buffer, send_sem, recv_sem
        )

    def total_of(buffer, count):
        terms = [buffer[index] for index in range(count)]
        while len(terms) > 1:
            terms = [sum(terms[index : index + 2]) for index in range(0, len(terms), 2)]
        return terms[0]

    def padded(face_couple, face_map):
        size = NRHS - FACE_CORNERS
        block = jnp.concatenate([face_couple, jnp.zeros((size, HALF), F32)], axis=0)
        row = jnp.concatenate([face_map, jnp.zeros((1, HALF - FACE_CORNERS), F32)], axis=1)
        return jnp.where(block_row == FACE_CORNERS, row, block)

    def coupling_of(block):
        return jnp.where(block_row < FACE_CORNERS, block, 0.0)

    def onehot_of(block):
        row = jnp.broadcast_to(block[FACE_CORNERS : FACE_CORNERS + 1, :128], (NRHS, 128))
        column = jnp.sum(jnp.where(diagonal, row, 0.0), axis=1, keepdims=True)
        hit = jnp.logical_and(column == corner_lane, corner_row < FACE_CORNERS)
        return jnp.where(hit, 1.0, 0.0)

    block_row = lax.broadcasted_iota(jnp.int32, (NRHS, HALF), 0)
    corner_row = lax.broadcasted_iota(jnp.int32, (NRHS, CORNERS), 0)
    corner_lane = lax.broadcasted_iota(jnp.int32, (NRHS, CORNERS), 1).astype(F32)
    diagonal = lax.broadcasted_iota(jnp.int32, (NRHS, 128), 0) == lax.broadcasted_iota(
        jnp.int32, (NRHS, 128), 1
    )
    lane = lax.broadcasted_iota(jnp.int32, (1, WIDTH), 1)
    lower_live = jnp.where(blk > 0, 1.0, 0.0).astype(F32)
    upper_live = jnp.where(blk < blk_count - 1, 1.0, 0.0).astype(F32)
    live = jnp.where(lane < HALF, lower_live, upper_live)

    small_loads[0].wait()
    small_loads[1].wait()
    couple_all = couple[0].astype(F32)
    map_all = corner_map[...].astype(F32)
    own_lower = padded(couple_all[:FACE_CORNERS], map_all[:, :FACE_CORNERS])
    own_upper = padded(couple_all[FACE_CORNERS:], map_all[:, FACE_CORNERS:])
    pl.semaphore_wait(barrier, len(greeted))
    send_faces(0, own_lower, own_upper)

    small_loads[2].wait()
    small_loads[3].wait()
    face_sign = signs[...].astype(F32) * live
    residual = live * rhs[0]

    def prec_product(values, wait):
        rounded = (face_sign * values).astype(BF16)
        total = None
        for index in range(BLOCKS):
            if wait:
                prec_loads[index].wait()
            span = slice(index * block_rows, (index + 1) * block_rows)
            part = lax.dot_general(
                rounded[:, span], prec[span, :], PLAIN, preferred_element_type=F32
            )
            total = part if total is None else total + part
        return total

    local_out = prec_product(residual, True)
    for load in late_loads:
        load.start()
    send_signed(1, face_sign * local_out)

    wait_faces(0)
    across_lower = face_in[0, 0]
    across_upper = face_in[0, 1]
    zeros = jnp.zeros((NRHS, HALF), F32)
    coupling = jnp.concatenate(
        [
            jnp.concatenate([coupling_of(own_lower), zeros], axis=1),
            jnp.concatenate([zeros, coupling_of(own_upper)], axis=1),
            jnp.concatenate([-coupling_of(across_lower), zeros], axis=1),
            jnp.concatenate([zeros, -coupling_of(across_upper)], axis=1),
        ],
        axis=0,
    ).astype(BF16)
    onehot = jnp.concatenate(
        [onehot_of(block) for block in (own_lower, own_upper, across_lower, across_upper)], axis=0
    ).astype(BF16)

    def combine(weights, values):
        return full_dot(weights.T, values, PLAIN)

    def reduce_all(turn, local_out, meanwhile):
        signed_out = face_sign * local_out
        face_turn = 1 + 2 * turn
        partial = narrow_dot(live * local_out, coupling, LAST)
        corner = narrow_dot(partial, onehot, PLAIN)
        for index, piece in enumerate(to_pieces(corner, spots)):
            pieces[turn, index] = piece
        scattered = exchange(
            spot_peer, spots, spot, lambda other: pieces.at[turn, other],
            gathered.at[turn], scatter_send.at[turn], scatter_recv.at[turn],
        )
        gathered[turn, spot] = pieces[turn, spot]
        precond = take_faces(face_turn, signed_out)
        scattered()
        along_y = spread(
            y_peer, ny, y, by_y.at[turn], y_send.at[turn], y_recv.at[turn],
            total_of(gathered.at[turn], spots),
        )
        signed_in = face_sign * precond
        if turn == 0:
            late_loads[0].wait()
        high, low = split(signed_in, 2)
        both = lax.dot_general(
            jnp.concatenate([high, low], axis=0), dual[...], PLAIN, preferred_element_type=F32
        )
        product, correction = both[:NRHS], both[NRHS:]
        grams = [
            full_dot(residual, precond, LAST),
            2.0 * full_dot(signed_in, product, LAST),
            2.0 * full_dot(signed_in, product if turn == 0 else product_old, LAST),
            jnp.zeros((NRHS, NRHS), F32),
        ]
        wide = jnp.concatenate(grams, axis=1)
        packed = jnp.concatenate([wide[:8], wide[8:]], axis=1)
        gram_at_spot = spread(
            spot_peer, spots, spot, gram_spot.at[turn], gram_send.at[turn], gram_recv.at[turn], packed
        )
        product_out = face_sign * (product if turn == 0 else product + correction)
        send_signed(face_turn + 1, product_out)
        along_y()
        along_z = spread(
            z_peer, nz, z, by_z.at[turn], z_send.at[turn], z_recv.at[turn],
            total_of(by_y.at[turn], ny),
        )
        gram_at_spot()
        gram_along_y = spread(
            y_peer, ny, y, gram_y.at[turn], gram_y_send.at[turn], gram_y_recv.at[turn],
            total_of(gram_spot.at[turn], spots),
        )
        between = meanwhile()
        gram_along_y()
        gram_along_z = spread(
            z_peer, nz, z, gram_z.at[turn], gram_z_send.at[turn], gram_z_recv.at[turn],
            total_of(gram_y.at[turn], ny),
        )
        along_z()
        gathered_back = spread(
            spot_peer, spots, spot, final.at[turn], final_send.at[turn], final_recv.at[turn],
            total_of(by_z.at[turn], nz),
        )
        if turn == 0:
            send_signed(CORRECTION, face_sign * correction)
        image = take_faces(face_turn + 1, product_out)
        gathered_back()
        corner = from_pieces([final[turn, index] for index in range(spots)])

        def take_grams():
            gram_along_z()
            total = total_of(gram_z.at[turn], nz)
            wide = jnp.concatenate([total[:, :64], total[:, 64:]], axis=0)
            return [wide[:, index * NRHS : (index + 1) * NRHS] for index in range(3)]

        return precond, product, image, face_sign * correction, corner, take_grams, between

    def prepare():
        late_loads[1].wait()
        high, middle, low = split(inverse[...], 3)
        inverse_high[...] = high
        inverse_low[...] = middle
        picked = lax.dot_general(onehot, high, PLAIN, preferred_element_type=F32)
        picked = picked + lax.dot_general(onehot, middle, PLAIN, preferred_element_type=F32)
        return picked + lax.dot_general(onehot, low, PLAIN, preferred_element_type=F32)

    def solve_corners(values):
        high, low = split(values, 2)
        both = lax.dot_general(
            jnp.concatenate([high, low], axis=0), inverse_high[...], PLAIN,
            preferred_element_type=F32,
        )
        cross = lax.dot_general(high, inverse_low[...], PLAIN, preferred_element_type=F32)
        return both[:NRHS] + (both[NRHS:] + cross)

    def coarse_image(corner):
        picked = full_dot(corner, inverse_rows, LAST)
        return face_sign * narrow_dot(picked, coupling, PLAIN)

    product_old = None
    direction, product_old, image_old, correction_old, corner_old, take_grams, inverse_rows = (
        reduce_all(0, local_out, prepare)
    )
    solved_old = solve_corners(corner_old)
    curve_coarse = 2.0 * full_dot(corner_old, solved_old, LAST)
    image_old = image_old + coarse_image(corner_old)
    gram_old, curve_old, _ = take_grams()
    curve_old = symmetric_part(curve_old + curve_coarse)
    alpha_old = spd_solve(curve_old, gram_old)
    residual = residual - combine(alpha_old, image_old)
    local_out = prec_product(residual, False)
    send_signed(3, face_sign * local_out)

    def invert():
        unit = lax.broadcasted_iota(jnp.int32, (NRHS, NRHS), 0) == lax.broadcasted_iota(
            jnp.int32, (NRHS, NRHS), 1
        )
        inverted = spd_solve(symmetric_part(gram_old), jnp.where(unit, 1.0, 0.0).astype(F32))
        return inverted, full_dot(inverted, full_dot(curve_old, inverted, PLAIN), PLAIN)

    precond, _, image, _, corner_new, take_grams, (gram_inverse, weight) = (
        reduce_all(1, local_out, invert)
    )
    solved_new = solve_corners(corner_new)
    curve_coarse = 2.0 * full_dot(corner_new, solved_new, LAST)
    cross_coarse = 2.0 * full_dot(corner_new, solved_old, LAST)
    image = image + coarse_image(corner_new)
    image_old = image_old + take_faces(CORRECTION, correction_old)
    gram_new, curve_new, cross = take_grams()
    beta = full_dot(gram_inverse, gram_new, PLAIN)
    inner = full_dot(
        jnp.concatenate([2.0 * (cross + cross_coarse), gram_new.T], axis=1),
        jnp.concatenate([gram_inverse, weight], axis=0),
        PLAIN,
    )
    curve = symmetric_part(curve_new + curve_coarse + full_dot(inner, gram_new, PLAIN))
    alpha = spd_solve(curve, gram_new)
    through = full_dot(beta, alpha, PLAIN)
    out_ref[0] = combine(
        jnp.concatenate([alpha_old + through, alpha], axis=0),
        jnp.concatenate([direction, precond], axis=0),
    )
    out_ref[1] = residual - combine(
        jnp.concatenate([through, alpha], axis=0), jnp.concatenate([image_old, image], axis=0)
    )
    for copy in drains:
        copy.wait_send()
    for turn in range(TURNS):
        for copy in face_copies(turn):
            copy.wait_send()


def extents(blk_count):
    return {192: (8, 12), 8: (2, 2), 4: (1, 2)}[blk_count]


def solution(mesh):
    blk_count, grp_count = mesh.shape["blk"], mesh.shape["grp"]
    ny, nz = extents(blk_count)
    spots = 2 * grp_count
    piece = (NRHS * CORNERS // 128 // spots, 128)
    dma = pltpu.SemaphoreType.DMA
    in_vmem = pl.BlockSpec(memory_space=pltpu.VMEM)
    in_place = pl.BlockSpec(memory_space=pl.ANY)

    def local(dual_rhs, dual_ops, prec_ops, corner_coupling, corner_map, signs, coarse_inverse):
        result = jax.ShapeDtypeStruct((1, NRHS, WIDTH), F32)
        both = pl.pallas_call(
            functools.partial(kernel, blk_count, grp_count, ny, nz),
            out_shape=jax.ShapeDtypeStruct((2, NRHS, WIDTH), F32),
            in_specs=[in_place] * 7,
            out_specs=in_vmem,
            scratch_shapes=[
                pltpu.VMEM((1, NRHS, WIDTH), F32),
                pltpu.VMEM((WIDTH, WIDTH), BF16),
                pltpu.VMEM((WIDTH, WIDTH), BF16),
                pltpu.VMEM((1, 2 * FACE_CORNERS, HALF), BF16),
                pltpu.VMEM((1, 2 * FACE_CORNERS), jnp.int32),
                pltpu.VMEM((1, WIDTH), jnp.int32),
                pltpu.VMEM((CORNERS, CORNERS), F32),
                pltpu.VMEM((CORNERS, CORNERS), BF16),
                pltpu.VMEM((CORNERS, CORNERS), BF16),
                pltpu.VMEM((TURNS, 2, NRHS, HALF), F32),
                pltpu.VMEM((TURNS, 2, NRHS, HALF), F32),
                pltpu.VMEM((2, spots, *piece), F32),
                pltpu.VMEM((2, spots, *piece), F32),
                pltpu.VMEM((2, ny, *piece), F32),
                pltpu.VMEM((2, nz, *piece), F32),
                pltpu.VMEM((2, spots, *piece), F32),
                pltpu.VMEM((2, spots, 8, 128), F32),
                pltpu.VMEM((2, ny, 8, 128), F32),
                pltpu.VMEM((2, nz, 8, 128), F32),
                dma((6,)),
                dma((BLOCKS,)),
                dma((TURNS, 2)),
                dma((TURNS, 2)),
                *[dma((2, count)) for count in (spots, ny, nz, spots, spots, ny, nz) for _ in range(2)],
            ],
            compiler_params=pltpu.CompilerParams(
                collective_id=0, has_side_effects=True, vmem_limit_bytes=67043328
            ),
            name="block_conjugate_gradients",
        )(
            dual_rhs, prec_ops.reshape(WIDTH, WIDTH), dual_ops.reshape(WIDTH, WIDTH),
            corner_coupling, corner_map, signs, coarse_inverse,
        )
        return both[:1], both[1:]

    in_specs = (
        P("grp", None, "blk"),
        P("grp", "blk", None),
        P("grp", "blk", None),
        P("grp", "blk", None),
        P("grp", "blk"),
        P("grp", "blk"),
        P(),
    )
    out_specs = (P("grp", None, "blk"), P("grp", None, "blk"))
    return jax.shard_map(local, mesh=mesh, in_specs=in_specs, out_specs=out_specs, check_vma=False)
```

```python
import functools

import jax
import jax.numpy as jnp
from jax import lax
from jax.experimental import pallas as pl
from jax.experimental.pallas import tpu as pltpu
from jax.sharding import PartitionSpec as P

F32 = jnp.float32
BF16 = jnp.bfloat16
HIGHEST = lax.Precision.HIGHEST
LAST = (((1,), (1,)), ((), ()))
PLAIN = (((1,), (0,)), ((), ()))
FIRST = (((0,), (0,)), ((), ()))
NRHS = 16
HALF = 512
WIDTH = 2 * HALF
FACE_CORNERS = 12
CORNERS = 768
BLOCKS = 4
TURNS = 6
CORRECTION = 5


def split(value, terms):
    parts = []
    for _ in range(terms):
        part = value.astype(BF16)
        parts.append(part)
        value = value - part.astype(F32)
    return parts


def narrow_dot(value, exact, dims, terms=3):
    rows = value.shape[0]
    stacked = jnp.concatenate(split(value, terms), axis=0)
    out = lax.dot_general(stacked, exact, dims, preferred_element_type=F32)
    total = out[:rows]
    for term in range(1, terms):
        total = total + out[term * rows : (term + 1) * rows]
    return total


def full_dot(left, right, dims):
    return lax.dot_general(left, right, dims, precision=HIGHEST, preferred_element_type=F32)


def to_pieces(corner, spots):
    tiles = [
        corner[8 * (index % 2) : 8 * (index % 2) + 8, 128 * (index // 2) : 128 * (index // 2) + 128]
        for index in range(NRHS * CORNERS // 1024)
    ]
    share = len(tiles) * 8 // spots
    if share % 8 == 0:
        many = share // 8
        return [
            jnp.concatenate(tiles[index * many : (index + 1) * many], axis=0)
            for index in range(spots)
        ]
    pieces = []
    for index in range(0, len(tiles), 3):
        first, middle, last = tiles[index : index + 3]
        pieces.append(jnp.concatenate([first, middle[:4]], axis=0))
        pieces.append(jnp.concatenate([last, middle[4:]], axis=0))
    return pieces


def from_pieces(pieces):
    tiles = []
    if pieces[0].shape[0] % 8 == 0:
        for piece in pieces:
            tiles += [piece[index : index + 8] for index in range(0, piece.shape[0], 8)]
    else:
        for first, last in zip(pieces[::2], pieces[1::2]):
            tiles += [first[:8], jnp.concatenate([first[8:], last[8:]], axis=0), last[:8]]
    columns = [
        jnp.concatenate(tiles[index : index + 2], axis=0) for index in range(0, len(tiles), 2)
    ]
    return jnp.concatenate(columns, axis=1)


def symmetric_part(matrix):
    return 0.5 * (matrix + matrix.T)


def spd_solve(matrix, target):
    size = matrix.shape[0]
    both = jnp.concatenate([matrix, target], axis=1)
    rows = lax.broadcasted_iota(jnp.int32, both.shape, 0)
    for k in range(size):
        column = jnp.broadcast_to(both[:, k : k + 1], both.shape)
        pivot_row = both[k : k + 1, :] / column[k : k + 1, :]
        both = jnp.where(rows == k, pivot_row, both - column * pivot_row)
    return both[:, size:]


def kernel(
    blk_count, grp_count, ny, nz,
    rhs_hbm, prec_hbm, dual_hbm, couple_hbm, map_hbm, sign_hbm, inverse_hbm,
    out_ref,
    rhs, prec, dual, couple, corner_map, signs, inverse, inverse_high, inverse_low,
    face_out, face_in, pieces, gathered, by_y, by_z, final, gram_spot, gram_y, gram_z,
    load_sem, prec_sem, face_send, face_recv,
    scatter_send, scatter_recv, y_send, y_recv, z_send, z_recv, final_send, final_recv,
    gram_send, gram_recv, gram_y_send, gram_y_recv, gram_z_send, gram_z_recv,
):
    small_loads = [
        pltpu.make_async_copy(source, target, load_sem.at[index])
        for index, (source, target) in enumerate(
            ((couple_hbm, couple), (map_hbm, corner_map), (rhs_hbm, rhs), (sign_hbm, signs))
        )
    ]
    block_rows = WIDTH // BLOCKS
    prec_loads = [
        pltpu.make_async_copy(
            prec_hbm.at[pl.ds(index * block_rows, block_rows)],
            prec.at[pl.ds(index * block_rows, block_rows)],
            prec_sem.at[index],
        )
        for index in range(BLOCKS)
    ]
    late_loads = [
        pltpu.make_async_copy(dual_hbm, dual, load_sem.at[4]),
        pltpu.make_async_copy(inverse_hbm, inverse, load_sem.at[5]),
    ]
    for load in small_loads + prec_loads:
        load.start()

    blk = lax.axis_index("blk")
    grp = lax.axis_index("grp")
    core = lax.rem(blk, 2)
    z = lax.rem(lax.div(blk, 2), nz)
    y = lax.div(blk, 2 * nz)
    spot = grp * 2 + core
    spots = 2 * grp_count

    def at(blk_index, grp_index):
        return {"blk": blk_index, "grp": grp_index}

    def spot_peer(step):
        other = lax.rem(spot + step, spots)
        return other, at(blk - core + lax.rem(other, 2), lax.div(other, 2))

    def y_peer(step):
        other = lax.rem(y + step, ny)
        return other, at(blk + (other - y) * (2 * nz), grp)

    def z_peer(step):
        other = lax.rem(z + step, nz)
        return other, at(blk + (other - z) * 2, grp)

    left = at(lax.rem(blk + blk_count - 1, blk_count), grp)
    right = at(lax.rem(blk + 1, blk_count), grp)

    barrier = pltpu.get_barrier_semaphore()
    greeted = [z_peer(step)[1] for step in range(1, nz)]
    greeted += [y_peer(step)[1] for step in range(1, ny)]
    greeted += [spot_peer(step)[1] for step in range(1, spots)]
    greeted += [left, right]
    for peer in greeted:
        pl.semaphore_signal(
            barrier, inc=1, device_id=peer, device_id_type=pl.DeviceIdType.MESH
        )

    def remote(source, target, send_sem, recv_sem, peer):
        return pltpu.make_async_remote_copy(
            src_ref=source,
            dst_ref=target,
            send_sem=send_sem,
            recv_sem=recv_sem,
            device_id=peer,
            device_id_type=pl.DeviceIdType.MESH,
        )

    def face_copies(turn):
        return (
            remote(
                face_out.at[turn, 0], face_in.at[turn, 1],
                face_send.at[turn, 0], face_recv.at[turn, 1], left,
            ),
            remote(
                face_out.at[turn, 1], face_in.at[turn, 0],
                face_send.at[turn, 1], face_recv.at[turn, 0], right,
            ),
        )

    def send_faces(turn, lower, upper):
        face_out[turn, 0] = lower
        face_out[turn, 1] = upper
        for copy in face_copies(turn):
            copy.start()

    def send_signed(turn, signed_out):
        send_faces(turn, signed_out[:, :HALF], signed_out[:, HALF:])

    def wait_faces(turn):
        for copy in face_copies(turn):
            copy.wait_recv()

    def take_faces(turn, signed_out):
        wait_faces(turn)
        partner = jnp.concatenate([face_in[turn, 0], face_in[turn, 1]], axis=1)
        return live * (signed_out + partner)

    drains = []

    def exchange(peer_of, count, own, source_of, buffer, send_sem, recv_sem):
        arrivals = []
        for step in range(1, count):
            other, peer = peer_of(step)
            send = remote(source_of(other), buffer.at[own], send_sem.at[other], recv_sem.at[own], peer)
            send.start()
            drains.append(send)
            arrivals.append(
                remote(source_of(other), buffer.at[other], send_sem.at[other], recv_sem.at[other], peer)
            )

        def arrive():
            for copy in arrivals:
                copy.wait_recv()

        return arrive

    def spread(peer_of, count, own, buffer, send_sem, recv_sem, value):
        buffer[own] = value
        return exchange(
            peer_of, count, own, lambda other: buffer.at[own], buffer, send_sem, recv_sem
        )

    def total_of(buffer, count):
        terms = [buffer[index] for index in range(count)]
        while len(terms) > 1:
            terms = [sum(terms[index : index + 2]) for index in range(0, len(terms), 2)]
        return terms[0]

    def padded(face_couple, face_map):
        size = NRHS - FACE_CORNERS
        block = jnp.concatenate([face_couple, jnp.zeros((size, HALF), F32)], axis=0)
        row = jnp.concatenate([face_map, jnp.zeros((1, HALF - FACE_CORNERS), F32)], axis=1)
        return jnp.where(block_row == FACE_CORNERS, row, block)

    def coupling_of(block):
        return jnp.where(block_row < FACE_CORNERS, block, 0.0)

    def onehot_of(block):
        row = jnp.broadcast_to(block[FACE_CORNERS : FACE_CORNERS + 1, :128], (NRHS, 128))
        column = jnp.sum(jnp.where(diagonal, row, 0.0), axis=1, keepdims=True)
        hit = jnp.logical_and(column == corner_lane, corner_row < FACE_CORNERS)
        return jnp.where(hit, 1.0, 0.0)

    block_row = lax.broadcasted_iota(jnp.int32, (NRHS, HALF), 0)
    corner_row = lax.broadcasted_iota(jnp.int32, (NRHS, CORNERS), 0)
    corner_lane = lax.broadcasted_iota(jnp.int32, (NRHS, CORNERS), 1).astype(F32)
    diagonal = lax.broadcasted_iota(jnp.int32, (NRHS, 128), 0) == lax.broadcasted_iota(
        jnp.int32, (NRHS, 128), 1
    )
    lane = lax.broadcasted_iota(jnp.int32, (1, WIDTH), 1)
    lower_live = jnp.where(blk > 0, 1.0, 0.0).astype(F32)
    upper_live = jnp.where(blk < blk_count - 1, 1.0, 0.0).astype(F32)
    live = jnp.where(lane < HALF, lower_live, upper_live)

    small_loads[0].wait()
    small_loads[1].wait()
    couple_all = couple[0].astype(F32)
    map_all = corner_map[...].astype(F32)
    own_lower = padded(couple_all[:FACE_CORNERS], map_all[:, :FACE_CORNERS])
    own_upper = padded(couple_all[FACE_CORNERS:], map_all[:, FACE_CORNERS:])
    pl.semaphore_wait(barrier, len(greeted))
    send_faces(0, own_lower, own_upper)

    small_loads[2].wait()
    small_loads[3].wait()
    face_sign = signs[...].astype(F32) * live
    residual = live * rhs[0]

    def prec_product(values, wait):
        rounded = (face_sign * values).astype(BF16)
        total = None
        for index in range(BLOCKS):
            if wait:
                prec_loads[index].wait()
            span = slice(index * block_rows, (index + 1) * block_rows)
            part = lax.dot_general(
                rounded[:, span], prec[span, :], PLAIN, preferred_element_type=F32
            )
            total = part if total is None else total + part
        return total

    local_out = prec_product(residual, True)
    for load in late_loads:
        load.start()
    send_signed(1, face_sign * local_out)

    wait_faces(0)
    across_lower = face_in[0, 0]
    across_upper = face_in[0, 1]
    zeros = jnp.zeros((NRHS, HALF), F32)
    coupling = jnp.concatenate(
        [
            jnp.concatenate([coupling_of(own_lower), zeros], axis=1),
            jnp.concatenate([zeros, coupling_of(own_upper)], axis=1),
            jnp.concatenate([-coupling_of(across_lower), zeros], axis=1),
            jnp.concatenate([zeros, -coupling_of(across_upper)], axis=1),
        ],
        axis=0,
    ).astype(BF16)
    onehot = jnp.concatenate(
        [onehot_of(block) for block in (own_lower, own_upper, across_lower, across_upper)], axis=0
    ).astype(BF16)

    def combine(weights, values):
        return full_dot(weights.T, values, PLAIN)

    def reduce_all(turn, local_out, meanwhile):
        signed_out = face_sign * local_out
        face_turn = 1 + 2 * turn
        partial = narrow_dot(live * local_out, coupling, LAST)
        corner = narrow_dot(partial, onehot, PLAIN)
        for index, piece in enumerate(to_pieces(corner, spots)):
            pieces[turn, index] = piece
        scattered = exchange(
            spot_peer, spots, spot, lambda other: pieces.at[turn, other],
            gathered.at[turn], scatter_send.at[turn], scatter_recv.at[turn],
        )
        gathered[turn, spot] = pieces[turn, spot]
        precond = take_faces(face_turn, signed_out)
        scattered()
        along_y = spread(
            y_peer, ny, y, by_y.at[turn], y_send.at[turn], y_recv.at[turn],
            total_of(gathered.at[turn], spots),
        )
        signed_in = face_sign * precond
        if turn == 0:
            late_loads[0].wait()
        high, low = split(signed_in, 2)
        both = lax.dot_general(
            jnp.concatenate([high, low], axis=0), dual[...], PLAIN, preferred_element_type=F32
        )
        product, correction = both[:NRHS], both[NRHS:]
        others = product if turn == 0 else jnp.concatenate([product, product_old], axis=0)
        grams = [full_dot(residual, precond, LAST), 2.0 * full_dot(signed_in, others, LAST)]
        grams.append(jnp.zeros((NRHS, 4 * NRHS - NRHS - others.shape[0]), F32))
        wide = jnp.concatenate(grams, axis=1)
        packed = jnp.concatenate([wide[:8], wide[8:]], axis=1)
        gram_at_spot = spread(
            spot_peer, spots, spot, gram_spot.at[turn], gram_send.at[turn], gram_recv.at[turn], packed
        )
        product_out = face_sign * (product if turn == 0 else product + correction)
        send_signed(face_turn + 1, product_out)
        along_y()
        along_z = spread(
            z_peer, nz, z, by_z.at[turn], z_send.at[turn], z_recv.at[turn],
            total_of(by_y.at[turn], ny),
        )
        gram_at_spot()
        gram_along_y = spread(
            y_peer, ny, y, gram_y.at[turn], gram_y_send.at[turn], gram_y_recv.at[turn],
            total_of(gram_spot.at[turn], spots),
        )
        between = meanwhile()
        gram_along_y()
        gram_along_z = spread(
            z_peer, nz, z, gram_z.at[turn], gram_z_send.at[turn], gram_z_recv.at[turn],
            total_of(gram_y.at[turn], ny),
        )
        along_z()
        gathered_back = spread(
            spot_peer, spots, spot, final.at[turn], final_send.at[turn], final_recv.at[turn],
            total_of(by_z.at[turn], nz),
        )
        if turn == 0:
            send_signed(CORRECTION, face_sign * correction)
        image = take_faces(face_turn + 1, product_out)
        gathered_back()
        corner = from_pieces([final[turn, index] for index in range(spots)])

        def take_grams():
            gram_along_z()
            total = total_of(gram_z.at[turn], nz)
            wide = jnp.concatenate([total[:, :64], total[:, 64:]], axis=0)
            return [wide[:, index * NRHS : (index + 1) * NRHS] for index in range(3)]

        return precond, product, image, face_sign * correction, corner, take_grams, between

    def prepare():
        late_loads[1].wait()
        high, low = split(inverse[...], 2)
        inverse_high[...] = high
        inverse_low[...] = low

    def solve_corners(values):
        high, low = split(values, 2)
        both = lax.dot_general(
            jnp.concatenate([high, low], axis=0), inverse_high[...], PLAIN,
            preferred_element_type=F32,
        )
        cross = lax.dot_general(high, inverse_low[...], PLAIN, preferred_element_type=F32)
        return both[:NRHS] + (both[NRHS:] + cross)

    def coarse_image(solved):
        picked = narrow_dot(solved, onehot, LAST)
        return face_sign * narrow_dot(picked, coupling, PLAIN)

    product_old = None
    direction, product_old, image_old, correction_old, corner_old, take_grams, _ = (
        reduce_all(0, local_out, prepare)
    )
    solved_old = solve_corners(corner_old)
    curve_coarse = 2.0 * full_dot(corner_old, solved_old, LAST)
    image_old = image_old + coarse_image(solved_old)
    gram_old, curve_old, _ = take_grams()
    curve_old = symmetric_part(curve_old + curve_coarse)
    alpha_old = spd_solve(curve_old, gram_old)
    residual = residual - combine(alpha_old, image_old)
    local_out = prec_product(residual, False)
    send_signed(3, face_sign * local_out)

    def invert():
        unit = lax.broadcasted_iota(jnp.int32, (NRHS, NRHS), 0) == lax.broadcasted_iota(
            jnp.int32, (NRHS, NRHS), 1
        )
        inverted = spd_solve(symmetric_part(gram_old), jnp.where(unit, 1.0, 0.0).astype(F32))
        return inverted, full_dot(inverted, full_dot(curve_old, inverted, PLAIN), PLAIN)

    precond, _, image, _, corner_new, take_grams, (gram_inverse, weight) = (
        reduce_all(1, local_out, invert)
    )
    solved_new = solve_corners(corner_new)
    curve_coarse = 2.0 * full_dot(corner_new, solved_new, LAST)
    cross_coarse = 2.0 * full_dot(corner_new, solved_old, LAST)
    image = image + coarse_image(solved_new)
    image_old = image_old + take_faces(CORRECTION, correction_old)
    gram_new, curve_new, cross = take_grams()
    beta = full_dot(gram_inverse, gram_new, PLAIN)
    inner = full_dot(
        jnp.concatenate([2.0 * (cross + cross_coarse), gram_new.T], axis=1),
        jnp.concatenate([gram_inverse, weight], axis=0),
        PLAIN,
    )
    curve = symmetric_part(curve_new + curve_coarse + full_dot(inner, gram_new, PLAIN))
    alpha = spd_solve(curve, gram_new)
    through = full_dot(beta, alpha, PLAIN)
    out_ref[0] = combine(
        jnp.concatenate([alpha_old + through, alpha], axis=0),
        jnp.concatenate([direction, precond], axis=0),
    )
    out_ref[1] = residual - combine(
        jnp.concatenate([through, alpha], axis=0), jnp.concatenate([image_old, image], axis=0)
    )
    for copy in drains:
        copy.wait_send()
    for turn in range(TURNS):
        for copy in face_copies(turn):
            copy.wait_send()


def extents(blk_count):
    return {192: (8, 12), 8: (2, 2), 4: (1, 2)}[blk_count]


def solution(mesh):
    blk_count, grp_count = mesh.shape["blk"], mesh.shape["grp"]
    ny, nz = extents(blk_count)
    spots = 2 * grp_count
    piece = (NRHS * CORNERS // 128 // spots, 128)
    dma = pltpu.SemaphoreType.DMA
    in_vmem = pl.BlockSpec(memory_space=pltpu.VMEM)
    in_place = pl.BlockSpec(memory_space=pl.ANY)

    def local(dual_rhs, dual_ops, prec_ops, corner_coupling, corner_map, signs, coarse_inverse):
        result = jax.ShapeDtypeStruct((1, NRHS, WIDTH), F32)
        both = pl.pallas_call(
            functools.partial(kernel, blk_count, grp_count, ny, nz),
            out_shape=jax.ShapeDtypeStruct((2, NRHS, WIDTH), F32),
            in_specs=[in_place] * 7,
            out_specs=in_vmem,
            scratch_shapes=[
                pltpu.VMEM((1, NRHS, WIDTH), F32),
                pltpu.VMEM((WIDTH, WIDTH), BF16),
                pltpu.VMEM((WIDTH, WIDTH), BF16),
                pltpu.VMEM((1, 2 * FACE_CORNERS, HALF), BF16),
                pltpu.VMEM((1, 2 * FACE_CORNERS), jnp.int32),
                pltpu.VMEM((1, WIDTH), jnp.int32),
                pltpu.VMEM((CORNERS, CORNERS), F32),
                pltpu.VMEM((CORNERS, CORNERS), BF16),
                pltpu.VMEM((CORNERS, CORNERS), BF16),
                pltpu.VMEM((TURNS, 2, NRHS, HALF), F32),
                pltpu.VMEM((TURNS, 2, NRHS, HALF), F32),
                pltpu.VMEM((2, spots, *piece), F32),
                pltpu.VMEM((2, spots, *piece), F32),
                pltpu.VMEM((2, ny, *piece), F32),
                pltpu.VMEM((2, nz, *piece), F32),
                pltpu.VMEM((2, spots, *piece), F32),
                pltpu.VMEM((2, spots, 8, 128), F32),
                pltpu.VMEM((2, ny, 8, 128), F32),
                pltpu.VMEM((2, nz, 8, 128), F32),
                dma((6,)),
                dma((BLOCKS,)),
                dma((TURNS, 2)),
                dma((TURNS, 2)),
                *[dma((2, count)) for count in (spots, ny, nz, spots, spots, ny, nz) for _ in range(2)],
            ],
            compiler_params=pltpu.CompilerParams(
                collective_id=0, has_side_effects=True, vmem_limit_bytes=67043328
            ),
            name="block_conjugate_gradients",
        )(
            dual_rhs, prec_ops.reshape(WIDTH, WIDTH), dual_ops.reshape(WIDTH, WIDTH),
            corner_coupling, corner_map, signs, coarse_inverse,
        )
        return both[:1], both[1:]

    in_specs = (
        P("grp", None, "blk"),
        P("grp", "blk", None),
        P("grp", "blk", None),
        P("grp", "blk", None),
        P("grp", "blk"),
        P("grp", "blk"),
        P(),
    )
    out_specs = (P("grp", None, "blk"), P("grp", None, "blk"))
    return jax.shard_map(local, mesh=mesh, in_specs=in_specs, out_specs=out_specs, check_vma=False)
```
